32 devices in a mesh: gz: 2 (over x), ax: 4 (over y, core), ay: 4 (over z).
Axes of the slice: x: 2, y: 2, z: 4, core: 2. Of those that a mesh axis runs over, the one named last changes fastest.
Arguments:
- source: float32 [64, 256, 512], P('gz', 'ax', 'ay'), may hold values from -120 to 120
- pressure: float32 [64, 256, 512], P('gz', 'ax', 'ay'), may hold values from -0.12 to 0.12
- storage: float32 [64, 256, 512], P('gz', 'ax', 'ay'), may hold values from 0.1 to 1
- trans_z: float32 [64, 256, 512], P('gz', 'ax', 'ay'), may hold values from 100 to 10000
- trans_x: float32 [64, 256, 512], P('gz', 'ax', 'ay'), may hold values from 0.3 to 3
- trans_y: float32 [64, 256, 512], P('gz', 'ax', 'ay'), may hold values from 0.3 to 3
Outputs:
- smoothed: float32 [64, 256, 512], P('gz', 'ax', 'ay')
- residual: float32 [64, 256, 512], P('gz', 'ax', 'ay')
The draws below stay inside these ranges and needn't reach their ends.
All inputs are finite; a program needn't handle non-finite values.
Results may differ from the reference program's by a relative error of at most 0.00035.
Values sent between devices are 32-bit elements; how exact they have to be, the bound alone decides.
No kernel may reach another device: no remote copies, remote signals or barrier semaphores. Data moves between devices by JAX's collectives and lax.ppermute only.
A program may use at most 128 MiB of HBM per device.

```python
import math
import jax
import jax.numpy as jnp
from jax import lax

SWEEPS = 2
NZ = 64
NX = 256
NY = 512


def draw_trans_z(key, part):
    fraction = jax.random.uniform(jax.random.fold_in(key, 17), (NZ, NX, NY), jnp.float32)
    lowest = math.log(100.0)
    highest = math.log(10000.0)
    values = jnp.exp(lowest + fraction * (highest - lowest))
    return jnp.clip(values, 100.0, 10000.0)


def level_of(key, extent, shards, low, largest):
    def one(axis_at, shards_of):
        heights = jax.random.uniform(jax.random.fold_in(jax.random.fold_in(key, 6), axis_at), (shards_of,), jnp.float32, low / len(shards), largest / len(shards))
        return jnp.repeat(jnp.exp(heights), extent[axis_at] // shards_of).reshape((-1,) + (1,) * (len(extent) - axis_at - 1))

    gain = one(*shards[0])
    for cut in shards[1:]:
        gain = gain * one(*cut)
    return gain


def scatter_about(key, shape, deviation, bound, shards=(), held_as=jnp.bfloat16):
    array = deviation * jax.random.normal(key, shape, jnp.float32)
    if shards:
        array = array * level_of(key, shape, shards, -0.22, 0.18)
    return jnp.clip(array, -bound, bound).astype(held_as)


def setup_inputs(seed: int = 0) -> dict:
    splits = jax.random.split(jax.random.key(seed), 7)
    source = scatter_about(splits[0], (NZ, NX, NY), 20.0, 120.0, ((0, 2), (1, 4), (2, 4)), jnp.float32)
    pressure = scatter_about(splits[1], (NZ, NX, NY), 0.02, 0.12, ((0, 2), (1, 4), (2, 4)), jnp.float32)
    storage = jnp.clip(jnp.exp(math.log(1.0) - 2.3025851 * jax.random.uniform(splits[2], (NZ, NX, NY), jnp.float32) ** level_of(splits[2], (NZ, NX, NY), ((0, 2), (1, 4), (2, 4)), -0.2, 0.2)), 0.1, 1.0)
    trans_z = draw_trans_z(jax.random.fold_in(splits[6], 71), 0)
    trans_x = jnp.clip(jnp.exp(math.log(3.0) - 2.3025851 * jax.random.uniform(splits[4], (NZ, NX, NY), jnp.float32) ** level_of(splits[4], (NZ, NX, NY), ((0, 2), (1, 4), (2, 4)), -0.2, 0.2)), 0.3, 3.0)
    trans_y = jnp.clip(jnp.exp(math.log(3.0) - 2.3025851 * jax.random.uniform(splits[5], (NZ, NX, NY), jnp.float32) ** level_of(splits[5], (NZ, NX, NY), ((0, 2), (1, 4), (2, 4)), -0.2, 0.2)), 0.3, 3.0)
    return dict(source=source, pressure=pressure, storage=storage, trans_z=trans_z, trans_x=trans_x, trans_y=trans_y)


OMEGA = 0.8

def shift_low(field, axis):
    size = field.shape[axis]
    zeros = jnp.zeros_like(lax.slice_in_dim(field, 0, 1, axis=axis))
    return jnp.concatenate([zeros, lax.slice_in_dim(field, 0, size - 1, axis=axis)], axis)

def shift_high(field, axis):
    size = field.shape[axis]
    zeros = jnp.zeros_like(lax.slice_in_dim(field, 0, 1, axis=axis))
    return jnp.concatenate([lax.slice_in_dim(field, 1, size, axis=axis), zeros], axis)

def line_solve(diag, upper, rhs):
    d_line = jnp.moveaxis(diag, 0, -1)
    du_line = -jnp.moveaxis(upper, 0, -1)
    dl_line = jnp.concatenate([jnp.zeros_like(du_line[..., :1]), du_line[..., :-1]], -1)
    b_line = jnp.moveaxis(rhs, 0, -1)[..., None]
    solution = lax.linalg.tridiagonal_solve(dl_line, d_line, du_line, b_line)[..., 0]
    return jnp.moveaxis(solution, -1, 0)

def reference(source, pressure, storage, trans_z, trans_x, trans_y):
    cz = trans_z * (lax.broadcasted_iota(jnp.int32, trans_z.shape, 0) < trans_z.shape[0] - 1).astype(trans_z.dtype)
    cx = trans_x * (lax.broadcasted_iota(jnp.int32, trans_x.shape, 1) < trans_x.shape[1] - 1).astype(trans_x.dtype)
    cy = trans_y * (lax.broadcasted_iota(jnp.int32, trans_y.shape, 2) < trans_y.shape[2] - 1).astype(trans_y.dtype)
    cz_b = shift_low(cz, 0)
    cx_w = shift_low(cx, 1)
    cy_w = shift_low(cy, 2)
    diag = storage + cz + cz_b + cx + cx_w + cy + cy_w
    field = pressure
    for sweep in range(SWEEPS):
        line = source + cx * shift_high(field, 1) + cx_w * shift_low(field, 1) + cy * shift_high(field, 2) + cy_w * shift_low(field, 2)
        solution = line_solve(diag, cz, line)
        field = field + OMEGA * (solution - field)
    applied = diag * field - cz * shift_high(field, 0) - cz_b * shift_low(field, 0)
    applied = applied - cx * shift_high(field, 1) - cx_w * shift_low(field, 1)
    applied = applied - cy * shift_high(field, 2) - cy_w * shift_low(field, 2)
    return (field, source - applied)
```

```python
import functools

import jax
import jax.numpy as jnp
from jax import lax
from jax.experimental import pallas as pl
from jax.experimental.pallas import tpu as pltpu
from jax.sharding import PartitionSpec as P

SWEEPS = 2
OMEGA = 0.8
SUB, LANES = 8, 128


def with_halo(cells, sides, width):
    for axis, dim in sides:
        count = lax.axis_size(axis)
        ends = count - 1
        head = lax.slice_in_dim(cells, 0, width, axis=dim)
        tail = lax.slice_in_dim(cells, cells.shape[dim] - width, cells.shape[dim], axis=dim)
        cells = jnp.concatenate(
            [
                lax.ppermute(tail, axis, [(i, (i + 1) % count) for i in range(ends)]),
                cells,
                lax.ppermute(head, axis, [((i + 1) % count, i) for i in range(ends)]),
            ],
            axis=dim,
        )
    return cells


def shifted(value, axis, steps):
    count = lax.axis_size(axis)
    leading, last = (max(0, -steps), min(count, count - steps))
    return lax.ppermute(value, axis, [(source, source + steps) for source in range(leading, last)])


def band_solve(diag, upper, lower, rhs):
    d_line = jnp.moveaxis(diag, 0, -1)
    du_line = jnp.moveaxis(upper, 0, -1)
    dl_line = jnp.moveaxis(lower, 0, -1)
    b_line = jnp.moveaxis(rhs, 0, -2)
    solution = lax.linalg.tridiagonal_solve(dl_line, d_line, du_line, b_line)
    return jnp.moveaxis(solution, -2, 0)


def edge_mask(field, axis, count, position):
    local = lax.broadcasted_iota(jnp.int32, field.shape, axis)
    width = field.shape[axis]
    total = width * count
    return (position * width + local < total - 1).astype(jnp.float32)


def areal_side(field, source, cx, cx_w, cy, cy_w):
    padded = with_halo(field, (("ax", 1), ("ay", 2)), 1)
    line = source + cx * padded[:, 2:, 1:-1] + cx_w * padded[:, :-2, 1:-1]
    return line + cy * padded[:, 1:-1, 2:] + cy_w * padded[:, 1:-1, :-2]


def many_blocks(source, pressure, storage, trans_z, trans_x, trans_y):
    cz = trans_z * edge_mask(trans_z, 0, lax.axis_size("gz"), lax.axis_index("gz"))
    cx = trans_x * edge_mask(trans_x, 1, lax.axis_size("ax"), lax.axis_index("ax"))
    cy = trans_y * edge_mask(trans_y, 2, lax.axis_size("ay"), lax.axis_index("ay"))
    below_face = shifted(cz[-1:], "gz", 1)
    west_face = shifted(cx[:, -1:], "ax", 1)
    south_face = shifted(cy[:, :, -1:], "ay", 1)
    cz_b = jnp.concatenate([below_face, cz[:-1]], 0)
    cx_w = jnp.concatenate([west_face, cx[:, :-1]], 1)
    cy_w = jnp.concatenate([south_face, cy[:, :, :-1]], 2)
    diag = storage + cz + cz_b + cx + cx_w + cy + cy_w
    field = pressure
    lower = -cz_b
    upper = -cz
    depth = diag.shape[0]
    inner_diag = diag[1:-1]
    inner_upper = upper[1:-1]
    inner_lower = lower[1:-1]
    blank = jnp.zeros_like(diag[: depth - 3])
    first_term = jnp.concatenate([lower[1:2], blank], 0)
    last_term = jnp.concatenate([blank, upper[depth - 2 : depth - 1]], 0)
    spikes = band_solve(
        inner_diag, inner_upper, inner_lower, jnp.stack([first_term, last_term], -1)
    )
    left_spike = spikes[..., 0]
    right_spike = spikes[..., 1]
    sub_pair = jnp.stack([lower[0], -lower[-1] * left_spike[-1]], 0)
    mid_pair = jnp.stack(
        [diag[0] - upper[0] * left_spike[0], diag[-1] - lower[-1] * right_spike[-1]], 0
    )
    sup_pair = jnp.stack([-upper[0] * right_spike[0], upper[-1]], 0)
    sub_all, mid_all, sup_all = (
        lax.all_gather(sub_pair, "gz", axis=0, tiled=True),
        lax.all_gather(mid_pair, "gz", axis=0, tiled=True),
        lax.all_gather(sup_pair, "gz", axis=0, tiled=True),
    )
    block = lax.axis_index("gz")
    for sweep in range(SWEEPS):
        line = areal_side(field, source, cx, cx_w, cy, cy_w)
        inner = band_solve(inner_diag, inner_upper, inner_lower, line[1:-1, :, :, None])[..., 0]
        side_pair = jnp.stack([line[0] - upper[0] * inner[0], line[-1] - lower[-1] * inner[-1]], 0)
        sides = lax.all_gather(side_pair, "gz", axis=0, tiled=True)
        reduced = band_solve(mid_all, sup_all, sub_all, sides[..., None])[..., 0]
        ends = lax.dynamic_slice_in_dim(reduced, 2 * block, 2, 0)
        middle = inner - left_spike * ends[0] - right_spike * ends[1]
        solution = jnp.concatenate([ends[:1], middle, ends[1:]], 0)
        field = field + OMEGA * (solution - field)
    padded = with_halo(field, (("gz", 0), ("ax", 1), ("ay", 2)), 1)
    applied = diag * field - cz * padded[2:, 1:-1, 1:-1] - cz_b * padded[:-2, 1:-1, 1:-1]
    applied = applied - cx * padded[1:-1, 2:, 1:-1] - cx_w * padded[1:-1, :-2, 1:-1]
    applied = applied - cy * padded[1:-1, 1:-1, 2:] - cy_w * padded[1:-1, 1:-1, :-2]
    return (field, source - applied)


def lane_iota():
    return lax.broadcasted_iota(jnp.int32, (SUB, LANES), 1)


def row_iota():
    return lax.broadcasted_iota(jnp.int32, (SUB, LANES), 0)


def rim_slot():
    return ((lane_iota() + 1) & (LANES - 1)) >> 1


def tiles_of(ref, z, groups):
    return [ref[z, SUB * x : SUB * (x + 1), :] for x in range(groups)]


def put_tiles(ref, z, tiles):
    for x, tile in enumerate(tiles):
        ref[z, SUB * x : SUB * (x + 1), :] = tile


def pack_layer(tiles, slot):
    out = tiles[0]
    for x, tile in enumerate(tiles[1:], 1):
        out = jnp.where(slot == x, pltpu.roll(tile, 2 * x, 1), out)
    return out


def unpack_layer(rim_tile, groups):
    return [rim_tile if x == 0 else pltpu.roll(rim_tile, LANES - 2 * x, 1) for x in range(groups)]


def join_rims(from_south, from_north, even):
    return jnp.where(even, pltpu.roll(from_south, 1, 1), pltpu.roll(from_north, LANES - 1, 1))


def pack_inputs_kernel(p_ref, tx_ref, ty_ref, rim_ref, east_ref, west_ref):
    depth, width, _ = p_ref.shape
    groups = width // SUB
    slot = rim_slot()
    for which, ref in enumerate((p_ref, ty_ref)):
        out = None
        for z in range(depth):
            part = pack_layer(tiles_of(ref, z, groups), slot)
            part = pltpu.roll(part, 2 * groups * z, 1) if z else part
            out = part if out is None else jnp.where(slot >= groups * z, part, out)
        rim_ref[which, 0] = out
    for z in range(depth):
        east_ref[0, z : z + 1, :] = p_ref[z, width - 1 : width, :]
        east_ref[1, z : z + 1, :] = tx_ref[z, SUB - 1 : SUB, :]
        west_ref[z : z + 1, :] = p_ref[z, 0:1, :]


def interior_couplings(tx, ty):
    rows = lax.broadcasted_iota(jnp.int32, tx.shape, 0)
    lanes = lax.broadcasted_iota(jnp.int32, tx.shape, 1)
    return (
        jnp.where(rows == tx.shape[0] - 1, 0.0, tx),
        jnp.where(lanes == tx.shape[1] - 1, 0.0, ty),
    )


def interior_inflow(p, cx, cy):
    width = p.shape[0]
    out = cx * pltpu.roll(p, width - 1, 0) + pltpu.roll(cx * p, 1, 0)
    return out + cy * pltpu.roll(p, LANES - 1, 1) + pltpu.roll(cy * p, 1, 1)


def prepare_kernel(source_ref, p_ref, storage_ref, tz_ref, tx_ref, ty_ref, s_ref, b_ref, cz_ref):
    def layer(z, _):
        cx, cy = interior_couplings(tx_ref[z], ty_ref[z])
        s_ref[z] = storage_ref[z] + cx + pltpu.roll(cx, 1, 0) + cy + pltpu.roll(cy, 1, 1)
        b_ref[z] = source_ref[z] + interior_inflow(p_ref[z], cx, cy)
        cz_ref[z] = tz_ref[z]
        return _

    lax.fori_loop(0, s_ref.shape[0], layer, 0, unroll=2)


def line_kernel(source_ref, p_ref, tx_ref, ty_ref, b_ref):
    def layer(z, _):
        cx, cy = interior_couplings(tx_ref[z], ty_ref[z])
        b_ref[z] = source_ref[z] + interior_inflow(p_ref[z], cx, cy)
        return _

    lax.fori_loop(0, b_ref.shape[0], layer, 0, unroll=2)


def split_rims(forward, backward, first_plane):
    return (
        jnp.where(first_plane, forward, backward),
        jnp.where(first_plane, backward, forward),
    )


def rim_at(rim_ref, z, groups):
    per = LANES // 2 // groups
    tile = rim_ref[z // per]
    shift = (LANES - 2 * groups * (z % per)) % LANES
    return unpack_layer(pltpu.roll(tile, shift, 1), groups)


def put_rim(rim_ref, z, tiles, slot):
    groups = len(tiles)
    per = LANES // 2 // groups
    tile = pltpu.roll(pack_layer(tiles, slot), 2 * groups * (z % per), 1)
    old = rim_ref[z // per]
    rim_ref[z // per] = jnp.where(slot // groups == z % per, tile, old)


def eliminate_kernel(
    s_ref, b_ref, cz_ref, own_rim_ref, own_east_ref, west_ref, east_ref, forward_ref, backward_ref,
    c_ref, inv_ref, d_ref, face_ref, rows_ref, rim_ref, add_rows, add_rim,
):
    depth, width, _ = s_ref.shape
    groups = width // SUB
    plane, ax, ay = lax.axis_index("gz"), lax.axis_index("ax"), lax.axis_index("ay")
    first = plane == 0
    lane, row = lane_iota(), row_iota()
    even = (lane & 1) == 0
    keep_west = jnp.where(ax > 0, 1.0, 0.0)
    keep_east = jnp.where(ax < lax.axis_size("ax") - 1, 1.0, 0.0)
    keep_south = jnp.where(ay > 0, 1.0, 0.0)
    keep_north = jnp.where(ay < lax.axis_size("ay") - 1, 1.0, 0.0)
    west = west_ref[1] * keep_west
    east = own_east_ref[1] * keep_east
    rows_ref[0] = west
    rows_ref[1] = east
    add_rows[0] = west * west_ref[0]
    add_rows[1] = east * east_ref[...]
    for t in range(rim_ref.shape[0]):
        south_p, north_p = split_rims(forward_ref[0, t], backward_ref[0, t], first)
        south_c, _ = split_rims(forward_ref[1, t], backward_ref[1, t], first)
        coupling = jnp.where(
            even, pltpu.roll(south_c, 1, 1) * keep_south, own_rim_ref[1, t] * keep_north
        )
        rim_ref[t] = coupling
        add_rim[t] = coupling * join_rims(south_p, north_p, even)
    rim_lane = (lane == 0) | (lane == LANES - 1)

    def sides(z):
        s, b = tiles_of(s_ref, z, groups), tiles_of(b_ref, z, groups)
        for x, (more_s, more_b) in enumerate(
            zip(rim_at(rim_ref, z, groups), rim_at(add_rim, z, groups))
        ):
            s[x] = s[x] + jnp.where(rim_lane, more_s, 0.0)
            b[x] = b[x] + jnp.where(rim_lane, more_b, 0.0)
        for x, which, at in ((0, 0, 0), (groups - 1, 1, SUB - 1)):
            s[x] = s[x] + jnp.where(row == at, rows_ref[which, pl.ds(z, 1), :], 0.0)
            b[x] = b[x] + jnp.where(row == at, add_rows[which, pl.ds(z, 1), :], 0.0)
        return s, b

    def step(k, carry):
        z = jnp.where(first, k, depth - 1 - k)
        ez = jnp.where(first, k, depth - 2 - k)
        q_prev, g_prev, c_prev = carry
        s, b = sides(z)
        e = tiles_of(cz_ref, ez, groups)
        q = [s[x] + c_prev[x] * q_prev[x] for x in range(groups)]
        g = [b[x] + c_prev[x] * g_prev[x] for x in range(groups)]
        inv = [1.0 / (q[x] + e[x]) for x in range(groups)]
        c = [e[x] * inv[x] for x in range(groups)]
        put_tiles(c_ref, z, c)
        put_tiles(inv_ref, z, inv)
        put_tiles(d_ref, z, [g[x] * inv[x] for x in range(groups)])
        return q, g, c

    zero = [jnp.zeros((SUB, LANES), jnp.float32) for _ in range(groups)]
    q, g, c = lax.fori_loop(0, depth - 1, step, (zero, zero, zero))
    s, b = sides(jnp.where(first, depth - 1, 0))
    put_tiles(face_ref, 0, [s[x] + c[x] * q[x] for x in range(groups)])
    put_tiles(face_ref, 1, [b[x] + c[x] * g[x] for x in range(groups)])
    face_ref[2] = cz_ref[depth - 1]


def back_kernel(c_ref, d_ref, p_ref, face_ref, other_ref, f_ref, coef_ref, rim_ref, ends_ref):
    depth, width, _ = p_ref.shape
    groups = width // SUB
    first = lax.axis_index("gz") == 0
    slot = rim_slot()
    q_a, q_b = face_ref[0], other_ref[0]
    e = jnp.where(first, face_ref[2], other_ref[2])
    det = 1.0 / (q_a * q_b + e * (q_a + q_b))
    coef_ref[0] = (q_b + e) * det
    coef_ref[1] = e * det
    coef_ref[2] = (q_a + e) * det
    coef_ref[3] = e
    x = coef_ref[0] * face_ref[1] + coef_ref[1] * other_ref[1]
    finish_back(x, c_ref, d_ref, p_ref, f_ref, rim_ref, ends_ref, first, slot)


def finish_back(x_end, c_ref, d_ref, p_ref, f_ref, rim_ref, ends_ref, first, slot):
    depth, width, _ = p_ref.shape
    groups = width // SUB

    def emit(z, x):
        f = []
        for t, p in enumerate(tiles_of(p_ref, z, groups)):
            f.append(p + OMEGA * (x[t] - p))
        put_tiles(f_ref, z, f)
        put_rim(rim_ref, z, f, slot)
        ends_ref[0, pl.ds(z, 1), :] = f[0][0:1, :]
        ends_ref[1, pl.ds(z, 1), :] = f[-1][SUB - 1 : SUB, :]

    def step(i, x):
        k = depth - 2 - i
        z = jnp.where(first, k, depth - 1 - k)
        c, d = tiles_of(c_ref, z, groups), tiles_of(d_ref, z, groups)
        x = [d[t] + c[t] * x[t] for t in range(groups)]
        emit(z, x)
        return x

    x = [x_end[SUB * t : SUB * (t + 1), :] for t in range(groups)]
    emit(jnp.where(first, depth - 1, 0), x)
    lax.fori_loop(0, depth - 1, step, x)


def eliminate_again_kernel(
    b_ref, c_ref, inv_ref, f_ref, rows_ref, rim_ref, west_ref, east_ref, forward_ref, backward_ref,
    d_ref, face_ref, add_rows, add_rim,
):
    depth, width, _ = b_ref.shape
    groups = width // SUB
    first = lax.axis_index("gz") == 0
    lane, row = lane_iota(), row_iota()
    even = (lane & 1) == 0
    add_rows[0] = rows_ref[0] * west_ref[...]
    add_rows[1] = rows_ref[1] * east_ref[...]
    for t in range(rim_ref.shape[0]):
        south, north = split_rims(forward_ref[t], backward_ref[t], first)
        add_rim[t] = rim_ref[t] * join_rims(south, north, even)
    rim_lane = (lane == 0) | (lane == LANES - 1)

    def side(z):
        b = tiles_of(b_ref, z, groups)
        for x, more in enumerate(rim_at(add_rim, z, groups)):
            b[x] = b[x] + jnp.where(rim_lane, more, 0.0)
        for x, which, at in ((0, 0, 0), (groups - 1, 1, SUB - 1)):
            b[x] = b[x] + jnp.where(row == at, add_rows[which, pl.ds(z, 1), :], 0.0)
        return b

    def step(k, g_prev):
        z = jnp.where(first, k, depth - 1 - k)
        b, inv, c = side(z), tiles_of(inv_ref, z, groups), tiles_of(c_ref, z, groups)
        g = [b[x] + g_prev[x] for x in range(groups)]
        put_tiles(d_ref, z, [g[x] * inv[x] for x in range(groups)])
        return [c[x] * g[x] for x in range(groups)]

    zero = [jnp.zeros((SUB, LANES), jnp.float32) for _ in range(groups)]
    carried = lax.fori_loop(0, depth - 1, step, zero)
    last = jnp.where(first, depth - 1, 0)
    b = side(last)
    put_tiles(face_ref, 0, [b[x] + carried[x] for x in range(groups)])
    face_ref[1] = f_ref[last]


def back_again_kernel(
    c_ref, d_ref, p_ref, coef_ref, face_ref, other_ref, f_ref, rim_ref, ends_ref, flux_ref
):
    first = lax.axis_index("gz") == 0
    slot = rim_slot()
    own, other = face_ref[0], other_ref[0]
    x = coef_ref[0] * own + coef_ref[1] * other
    y = coef_ref[2] * other + coef_ref[1] * own
    mine, theirs = face_ref[1], other_ref[1]
    mine = mine + OMEGA * (x - mine)
    theirs = theirs + OMEGA * (y - theirs)
    flux_ref[...] = coef_ref[3] * (mine - theirs)
    finish_back(x, c_ref, d_ref, p_ref, f_ref, rim_ref, ends_ref, first, slot)


def residual_kernel(source_ref, storage_ref, tz_ref, tx_ref, ty_ref, f_ref, flux_ref, r_ref):
    chunk, width, _ = r_ref.shape
    depth = f_ref.shape[0]
    start = pl.program_id(0) * chunk
    first = lax.axis_index("gz") == 0

    def layer(i, below):
        z = start + i
        p = f_ref[z]
        cx, cy = interior_couplings(tx_ref[i], ty_ref[i])
        above = tz_ref[z] * (p - f_ref[jnp.minimum(z + 1, depth - 1)])
        gx = cx * (p - pltpu.roll(p, width - 1, 0))
        gy = cy * (p - pltpu.roll(p, LANES - 1, 1))
        r = source_ref[i] - storage_ref[i] * p - (gx - pltpu.roll(gx, 1, 0))
        r_ref[i] = r - (gy - pltpu.roll(gy, 1, 1)) - (above - below)
        return above

    under = jnp.maximum(start - 1, 0)
    below = tz_ref[under] * (f_ref[under] - f_ref[start])
    lax.fori_loop(0, chunk, layer, below, unroll=2)
    end = jnp.where(first, depth - 1, 0)

    @pl.when((end >= start) & (end < start + chunk))
    def _():
        r_ref[end - start] = r_ref[end - start] - flux_ref[...]


def rims_kernel(
    r_ref, rows_ref, rim_ref, own_ref, ends_ref, west_ref, east_ref, forward_ref, backward_ref, out_ref
):
    depth, width, _ = r_ref.shape
    groups = width // SUB
    first = lax.axis_index("gz") == 0
    lane, row = lane_iota(), row_iota()
    even = (lane & 1) == 0
    rim_lane = (lane == 0) | (lane == LANES - 1)
    south, north = split_rims(forward_ref[0], backward_ref[0], first)
    more = rim_ref[0] * (join_rims(south, north, even) - own_ref[0])
    west = rows_ref[0] * (west_ref[...] - ends_ref[0])
    east = rows_ref[1] * (east_ref[...] - ends_ref[1])
    for z in range(depth):
        tiles = tiles_of(r_ref, z, groups)
        moved = pltpu.roll(more, (LANES - 2 * groups * z) % LANES, 1) if z else more
        for x, part in enumerate(unpack_layer(moved, groups)):
            tiles[x] = tiles[x] + jnp.where(rim_lane, part, 0.0)
        tiles[0] = tiles[0] + jnp.where(row == 0, west[z : z + 1, :], 0.0)
        tiles[-1] = tiles[-1] + jnp.where(row == SUB - 1, east[z : z + 1, :], 0.0)
        put_tiles(out_ref, z, tiles)


def ring(value, axis, step):
    count = lax.axis_size(axis)
    return lax.ppermute(value, axis, [(i, (i + step) % count) for i in range(count)])


def snake(value, step):
    count = lax.axis_size("ay")
    order = list(range(count)) + [2 * count - 1 - i for i in range(count)]
    total = len(order)
    pairs = [(order[i], order[(i + step) % total]) for i in range(total)]
    return lax.ppermute(value, ("gz", "ay"), pairs)


def two_blocks(source, pressure, storage, trans_z, trans_x, trans_y):
    depth, width, length = pressure.shape
    groups = width // SUB
    chunk = LANES // 2 // groups
    steps = depth // chunk
    f32 = jnp.float32

    def shape(*dims):
        return jax.ShapeDtypeStruct(dims, f32)

    block = shape(depth, width, length)
    face = shape(width, length)
    rim = shape(steps, SUB, LANES)
    ends = shape(2, depth, length)
    whole = pl.BlockSpec(memory_space=pltpu.VMEM)
    part = pl.BlockSpec((chunk, width, length), lambda i: (i, 0, 0))
    part_rim = pl.BlockSpec((1, SUB, LANES), lambda i: (i, 0, 0))
    part_ends = pl.BlockSpec((2, chunk, length), lambda i: (0, i, 0))
    part_end = pl.BlockSpec((chunk, length), lambda i: (i, 0))

    def cost(flops, nbytes):
        return pl.CostEstimate(flops=flops, bytes_accessed=nbytes, transcendentals=0)

    size = depth * width * length

    rims, east, west = pl.pallas_call(
        pack_inputs_kernel,
        grid=(steps,),
        in_specs=[part, pl.BlockSpec((chunk, SUB, length), lambda i: (i, groups - 1, 0)), part],
        out_specs=[
            pl.BlockSpec((2, 1, SUB, LANES), lambda i: (0, i, 0, 0)),
            part_ends,
            part_end,
        ],
        out_shape=[shape(2, steps, SUB, LANES), ends, shape(depth, length)],
        cost_estimate=cost(4 * size, 8 * size),
        name="pack_inputs",
    )(pressure, trans_x, trans_y)

    from_west = ring(east, "ax", 1)
    from_east = ring(west, "ax", -1)
    forward = snake(rims, 1)
    backward = snake(rims, -1)

    s, b, cz = pl.pallas_call(
        prepare_kernel,
        grid=(steps,),
        in_specs=[part] * 6,
        out_specs=[part] * 3,
        out_shape=[block] * 3,
        cost_estimate=cost(20 * size, 36 * size),
        name="prepare",
    )(source, pressure, storage, trans_z, trans_x, trans_y)

    scratch = [pltpu.VMEM((2, depth, length), f32), pltpu.VMEM((steps, SUB, LANES), f32)]
    c, inv, d, faces, rows, coupling = pl.pallas_call(
        eliminate_kernel,
        in_specs=[whole] * 9,
        out_specs=[whole] * 6,
        out_shape=[block, block, block, shape(3, width, length), ends, rim],
        scratch_shapes=scratch,
        cost_estimate=cost(30 * size, 24 * size),
        name="eliminate",
    )(s, b, cz, rims, east, from_west, from_east, forward, backward)

    others = ring(faces, "gz", 1)
    field, coefs, rims, edges = pl.pallas_call(
        back_kernel,
        in_specs=[whole] * 5,
        out_specs=[whole] * 4,
        out_shape=[block, shape(4, width, length), rim, ends],
        cost_estimate=cost(10 * size, 16 * size),
        name="back",
    )(c, d, pressure, faces, others)

    from_west = ring(edges[1], "ax", 1)
    from_east = ring(edges[0], "ax", -1)
    forward = snake(rims, 1)
    backward = snake(rims, -1)

    b = pl.pallas_call(
        line_kernel,
        grid=(steps,),
        in_specs=[part] * 4,
        out_specs=part,
        out_shape=block,
        cost_estimate=cost(16 * size, 20 * size),
        name="line",
    )(source, field, trans_x, trans_y)

    d, faces = pl.pallas_call(
        eliminate_again_kernel,
        in_specs=[whole] * 10,
        out_specs=[whole] * 2,
        out_shape=[block, shape(2, width, length)],
        scratch_shapes=scratch,
        cost_estimate=cost(10 * size, 16 * size),
        name="eliminate_again",
    )(b, c, inv, field, rows, coupling, from_west, from_east, forward, backward)

    others = ring(faces, "gz", 1)
    field, rims, edges, flux = pl.pallas_call(
        back_again_kernel,
        in_specs=[whole] * 6,
        out_specs=[whole] * 4,
        out_shape=[block, rim, ends, face],
        cost_estimate=cost(10 * size, 16 * size),
        name="back_again",
    )(c, d, field, coefs, faces, others)

    from_west = ring(edges[1], "ax", 1)
    from_east = ring(edges[0], "ax", -1)
    forward = snake(rims, 1)
    backward = snake(rims, -1)

    r = pl.pallas_call(
        residual_kernel,
        grid=(steps,),
        in_specs=[part, part, whole, part, part, whole, whole],
        out_specs=part,
        out_shape=block,
        cost_estimate=cost(20 * size, 28 * size),
        name="residual",
    )(source, storage, trans_z, trans_x, trans_y, field, flux)

    r = pl.pallas_call(
        rims_kernel,
        grid=(steps,),
        in_specs=[
            part, part_ends, part_rim, part_rim, part_ends, part_end, part_end, part_rim, part_rim
        ],
        out_specs=part,
        out_shape=block,
        cost_estimate=cost(4 * size, 8 * size),
        name="rims",
    )(r, rows, coupling, rims, edges, from_west, from_east, forward, backward)
    return field, r


def body(*args):
    depth, width, length = args[0].shape
    groups = width // SUB
    fits = width % SUB == 0 and length == LANES and LANES // 2 % groups == 0
    if lax.axis_size("gz") == 2 and fits and depth % (LANES // 2 // groups) == 0:
        return two_blocks(*args)
    return many_blocks(*args)


def solution(mesh):
    spec = P("gz", "ax", "ay")
    return jax.shard_map(
        body, mesh=mesh, in_specs=(spec,) * 6, out_specs=(spec, spec), check_vma=False
    )
```

```python
import functools

import jax
import jax.numpy as jnp
from jax import lax
from jax.experimental import pallas as pl
from jax.experimental.pallas import tpu as pltpu
from jax.sharding import PartitionSpec as P

SWEEPS = 2
OMEGA = 0.8
SUB, LANES = 8, 128
LIMIT = 16 << 20


def with_halo(cells, sides, width):
    for axis, dim in sides:
        count = lax.axis_size(axis)
        ends = count - 1
        head = lax.slice_in_dim(cells, 0, width, axis=dim)
        tail = lax.slice_in_dim(cells, cells.shape[dim] - width, cells.shape[dim], axis=dim)
        cells = jnp.concatenate(
            [
                lax.ppermute(tail, axis, [(i, (i + 1) % count) for i in range(ends)]),
                cells,
                lax.ppermute(head, axis, [((i + 1) % count, i) for i in range(ends)]),
            ],
            axis=dim,
        )
    return cells


def shifted(value, axis, steps):
    count = lax.axis_size(axis)
    leading, last = (max(0, -steps), min(count, count - steps))
    return lax.ppermute(value, axis, [(source, source + steps) for source in range(leading, last)])


def band_solve(diag, upper, lower, rhs):
    d_line = jnp.moveaxis(diag, 0, -1)
    du_line = jnp.moveaxis(upper, 0, -1)
    dl_line = jnp.moveaxis(lower, 0, -1)
    b_line = jnp.moveaxis(rhs, 0, -2)
    solution = lax.linalg.tridiagonal_solve(dl_line, d_line, du_line, b_line)
    return jnp.moveaxis(solution, -2, 0)


def edge_mask(field, axis, count, position):
    local = lax.broadcasted_iota(jnp.int32, field.shape, axis)
    width = field.shape[axis]
    total = width * count
    return (position * width + local < total - 1).astype(jnp.float32)


def areal_side(field, source, cx, cx_w, cy, cy_w):
    padded = with_halo(field, (("ax", 1), ("ay", 2)), 1)
    line = source + cx * padded[:, 2:, 1:-1] + cx_w * padded[:, :-2, 1:-1]
    return line + cy * padded[:, 1:-1, 2:] + cy_w * padded[:, 1:-1, :-2]


def many_blocks(source, pressure, storage, trans_z, trans_x, trans_y):
    cz = trans_z * edge_mask(trans_z, 0, lax.axis_size("gz"), lax.axis_index("gz"))
    cx = trans_x * edge_mask(trans_x, 1, lax.axis_size("ax"), lax.axis_index("ax"))
    cy = trans_y * edge_mask(trans_y, 2, lax.axis_size("ay"), lax.axis_index("ay"))
    below_face = shifted(cz[-1:], "gz", 1)
    west_face = shifted(cx[:, -1:], "ax", 1)
    south_face = shifted(cy[:, :, -1:], "ay", 1)
    cz_b = jnp.concatenate([below_face, cz[:-1]], 0)
    cx_w = jnp.concatenate([west_face, cx[:, :-1]], 1)
    cy_w = jnp.concatenate([south_face, cy[:, :, :-1]], 2)
    diag = storage + cz + cz_b + cx + cx_w + cy + cy_w
    field = pressure
    lower = -cz_b
    upper = -cz
    depth = diag.shape[0]
    inner_diag = diag[1:-1]
    inner_upper = upper[1:-1]
    inner_lower = lower[1:-1]
    blank = jnp.zeros_like(diag[: depth - 3])
    first_term = jnp.concatenate([lower[1:2], blank], 0)
    last_term = jnp.concatenate([blank, upper[depth - 2 : depth - 1]], 0)
    spikes = band_solve(
        inner_diag, inner_upper, inner_lower, jnp.stack([first_term, last_term], -1)
    )
    left_spike = spikes[..., 0]
    right_spike = spikes[..., 1]
    sub_pair = jnp.stack([lower[0], -lower[-1] * left_spike[-1]], 0)
    mid_pair = jnp.stack(
        [diag[0] - upper[0] * left_spike[0], diag[-1] - lower[-1] * right_spike[-1]], 0
    )
    sup_pair = jnp.stack([-upper[0] * right_spike[0], upper[-1]], 0)
    sub_all, mid_all, sup_all = (
        lax.all_gather(sub_pair, "gz", axis=0, tiled=True),
        lax.all_gather(mid_pair, "gz", axis=0, tiled=True),
        lax.all_gather(sup_pair, "gz", axis=0, tiled=True),
    )
    block = lax.axis_index("gz")
    for sweep in range(SWEEPS):
        line = areal_side(field, source, cx, cx_w, cy, cy_w)
        inner = band_solve(inner_diag, inner_upper, inner_lower, line[1:-1, :, :, None])[..., 0]
        side_pair = jnp.stack([line[0] - upper[0] * inner[0], line[-1] - lower[-1] * inner[-1]], 0)
        sides = lax.all_gather(side_pair, "gz", axis=0, tiled=True)
        reduced = band_solve(mid_all, sup_all, sub_all, sides[..., None])[..., 0]
        ends = lax.dynamic_slice_in_dim(reduced, 2 * block, 2, 0)
        middle = inner - left_spike * ends[0] - right_spike * ends[1]
        solution = jnp.concatenate([ends[:1], middle, ends[1:]], 0)
        field = field + OMEGA * (solution - field)
    padded = with_halo(field, (("gz", 0), ("ax", 1), ("ay", 2)), 1)
    applied = diag * field - cz * padded[2:, 1:-1, 1:-1] - cz_b * padded[:-2, 1:-1, 1:-1]
    applied = applied - cx * padded[1:-1, 2:, 1:-1] - cx_w * padded[1:-1, :-2, 1:-1]
    applied = applied - cy * padded[1:-1, 1:-1, 2:] - cy_w * padded[1:-1, 1:-1, :-2]
    return (field, source - applied)


def lane_iota():
    return lax.broadcasted_iota(jnp.int32, (SUB, LANES), 1)


def row_iota():
    return lax.broadcasted_iota(jnp.int32, (SUB, LANES), 0)


def rim_slot():
    return ((lane_iota() + 1) & (LANES - 1)) >> 1


def tiles_of(ref, z, groups):
    return [ref[z, SUB * x : SUB * (x + 1), :] for x in range(groups)]


def put_tiles(ref, z, tiles):
    for x, tile in enumerate(tiles):
        ref[z, SUB * x : SUB * (x + 1), :] = tile


def join_rims(from_south, from_north, even):
    return jnp.where(even, pltpu.roll(from_south, 1, 1), pltpu.roll(from_north, LANES - 1, 1))


def pack_chunk(ref, start, slot, groups):
    out = None
    for z in range(LANES // 2 // groups):
        for x in range(groups):
            m = groups * z + x
            tile = ref[start + z, SUB * x : SUB * (x + 1), :]
            tile = pltpu.roll(tile, 2 * m, 1) if m else tile
            out = tile if out is None else jnp.where(slot == m, tile, out)
    return out


def copies(pairs, sems):
    return [pltpu.make_async_copy(src, dst, sems.at[i]) for i, (src, dst) in enumerate(pairs)]


def pack_inputs_kernel(p_hbm, tx_hbm, ty_hbm, rim_ref, east_ref, west_ref, p_ref, tx_ref, ty_ref, sems):
    depth, width, _ = p_ref.shape
    groups = width // SUB
    slot = rim_slot()
    chunk = LANES // 2 // groups
    steps = depth // chunk
    parts = [slice(i * chunk, (i + 1) * chunk) for i in range(steps)]
    pairs = [(h.at[at], v.at[at]) for at in parts for h, v in ((p_hbm, p_ref), (ty_hbm, ty_ref))]
    moves = copies(pairs + [(tx_hbm, tx_ref)], sems)
    for move in moves:
        move.start()
    for i in range(steps):
        for which, ref in enumerate((p_ref, ty_ref)):
            moves[2 * i + which].wait()
            rim_ref[which, i] = pack_chunk(ref, i * chunk, slot, groups)
    moves[-1].wait()
    for z in range(depth):
        east_ref[0, z : z + 1, :] = p_ref[z, width - 1 : width, :]
        east_ref[1, z : z + 1, :] = tx_ref[z, width - 1 : width, :]
        west_ref[z : z + 1, :] = p_ref[z, 0:1, :]


def interior_couplings(tx, ty):
    rows = lax.broadcasted_iota(jnp.int32, tx.shape, 0)
    lanes = lax.broadcasted_iota(jnp.int32, tx.shape, 1)
    return (
        jnp.where(rows == tx.shape[0] - 1, 0.0, tx),
        jnp.where(lanes == tx.shape[1] - 1, 0.0, ty),
    )


def interior_inflow(p, cx, cy):
    width = p.shape[0]
    out = cx * pltpu.roll(p, width - 1, 0) + pltpu.roll(cx * p, 1, 0)
    return out + cy * pltpu.roll(p, LANES - 1, 1) + pltpu.roll(cy * p, 1, 1)


def prepare_kernel(
    source_hbm, storage_hbm, tz_hbm, p_ref, tx_ref, ty_ref,
    s_ref, b_ref, source_ref, storage_ref, tz_ref, sems,
):
    depth = s_ref.shape[0]
    steps = (sems.shape[0] - 1) // 2
    chunk = depth // steps
    parts = [slice(i * chunk, (i + 1) * chunk) for i in range(steps)]
    pairs = [
        (h.at[at], v.at[at])
        for at in parts
        for h, v in ((storage_hbm, storage_ref), (source_hbm, source_ref))
    ]
    moves = copies(pairs + [(tz_hbm, tz_ref)], sems)
    for move in moves:
        move.start()

    def layer(z, _):
        cx, cy = interior_couplings(tx_ref[z], ty_ref[z])
        s_ref[z] = storage_ref[z] + cx + pltpu.roll(cx, 1, 0) + cy + pltpu.roll(cy, 1, 1)
        b_ref[z] = source_ref[z] + interior_inflow(p_ref[z], cx, cy)
        return _

    for i in range(steps):
        moves[2 * i].wait()
        moves[2 * i + 1].wait()
        lax.fori_loop(i * chunk, (i + 1) * chunk, layer, 0, unroll=4)
    moves[-1].wait()


def line_kernel(source_ref, p_ref, tx_ref, ty_ref, b_ref):
    def layer(z, _):
        cx, cy = interior_couplings(tx_ref[z], ty_ref[z])
        b_ref[z] = source_ref[z] + interior_inflow(p_ref[z], cx, cy)
        return _

    lax.fori_loop(0, b_ref.shape[0], layer, 0, unroll=4)


def split_rims(forward, backward, first_plane):
    return (
        jnp.where(first_plane, forward, backward),
        jnp.where(first_plane, backward, forward),
    )


def rim_part(tile, inner, x, groups):
    return pltpu.roll(tile, (LANES - 2 * x - 2 * groups * inner) % LANES, 1)


def chunked(depth, groups, first, body, carry):
    per = LANES // 2 // groups
    steps = depth // per

    def step(i, carry):
        chunk = jnp.where(first, i, steps - 1 - i)
        inner = [jnp.where(first, j, per - 1 - j) for j in range(per)]
        return body(chunk, [(chunk * per + at, at) for at in inner], carry)

    return lax.fori_loop(0, steps, step, carry)


def eliminate_kernel(
    s_ref, b_ref, cz_ref, own_rim_ref, own_east_ref, west_ref, east_ref, forward_ref, backward_ref,
    c_ref, inv_ref, d_ref, face_ref, rows_ref, rim_ref, add_rows, add_rim,
):
    depth, width, _ = s_ref.shape
    groups = width // SUB
    plane, ax, ay = lax.axis_index("gz"), lax.axis_index("ax"), lax.axis_index("ay")
    first = plane == 0
    lane, row = lane_iota(), row_iota()
    even = (lane & 1) == 0
    keep_west = jnp.where(ax > 0, 1.0, 0.0)
    keep_east = jnp.where(ax < lax.axis_size("ax") - 1, 1.0, 0.0)
    keep_south = jnp.where(ay > 0, 1.0, 0.0)
    keep_north = jnp.where(ay < lax.axis_size("ay") - 1, 1.0, 0.0)
    west = west_ref[1] * keep_west
    east = own_east_ref[1] * keep_east
    rows_ref[0] = west
    rows_ref[1] = east
    add_rows[0] = west * west_ref[0]
    add_rows[1] = east * east_ref[...]
    for t in range(rim_ref.shape[0]):
        south_p, north_p = split_rims(forward_ref[0, t], backward_ref[0, t], first)
        south_c, _ = split_rims(forward_ref[1, t], backward_ref[1, t], first)
        coupling = jnp.where(
            even, pltpu.roll(south_c, 1, 1) * keep_south, own_rim_ref[1, t] * keep_north
        )
        rim_ref[t] = coupling
        add_rim[t] = coupling * join_rims(south_p, north_p, even)
    rim_lane = (lane == 0) | (lane == LANES - 1)

    def body(chunk, layers, carry):
        tile_s, tile_b = rim_ref[chunk], add_rim[chunk]
        q, g, c = carry
        for z, inner in layers:
            ez = jnp.maximum(jnp.where(first, z, z - 1), 0)
            s, b = tiles_of(s_ref, z, groups), tiles_of(b_ref, z, groups)
            for x in range(groups):
                s[x] = s[x] + jnp.where(rim_lane, rim_part(tile_s, inner, x, groups), 0.0)
                b[x] = b[x] + jnp.where(rim_lane, rim_part(tile_b, inner, x, groups), 0.0)
            for x, which, at in ((0, 0, 0), (groups - 1, 1, SUB - 1)):
                s[x] = s[x] + jnp.where(row == at, rows_ref[which, pl.ds(z, 1), :], 0.0)
                b[x] = b[x] + jnp.where(row == at, add_rows[which, pl.ds(z, 1), :], 0.0)
            e = tiles_of(cz_ref, ez, groups)
            q = [s[x] + c[x] * q[x] for x in range(groups)]
            g = [b[x] + c[x] * g[x] for x in range(groups)]
            inv = [1.0 / (q[x] + e[x]) for x in range(groups)]
            c = [e[x] * inv[x] for x in range(groups)]
            put_tiles(c_ref, z, c)
            put_tiles(inv_ref, z, inv)
            put_tiles(d_ref, z, [g[x] * inv[x] for x in range(groups)])
        return q, g, c

    zero = [jnp.zeros((SUB, LANES), jnp.float32) for _ in range(groups)]
    q, g, _ = chunked(depth, groups, first, body, (zero, zero, zero))
    put_tiles(face_ref, 0, q)
    put_tiles(face_ref, 1, g)
    face_ref[2] = cz_ref[depth - 1]


def back_kernel(c_ref, d_ref, p_ref, face_ref, other_ref, f_ref, coef_ref, rim_ref, ends_ref):
    depth, width, _ = p_ref.shape
    groups = width // SUB
    first = lax.axis_index("gz") == 0
    slot = rim_slot()
    q_a, q_b = face_ref[0], other_ref[0]
    e = jnp.where(first, face_ref[2], other_ref[2])
    det = 1.0 / (q_a * q_b + e * (q_a + q_b))
    coef_ref[0] = (q_b + e) * det
    coef_ref[1] = e * det
    coef_ref[2] = (q_a + e) * det
    coef_ref[3] = e
    x = coef_ref[0] * face_ref[1] + coef_ref[1] * other_ref[1]
    finish_back(x, c_ref, d_ref, p_ref, f_ref, rim_ref, ends_ref, first, slot)


def finish_back(x_end, c_ref, d_ref, p_ref, f_ref, rim_ref, ends_ref, first, slot):
    depth, width, _ = p_ref.shape
    groups = width // SUB

    def body(chunk, layers, x):
        out = jnp.zeros((SUB, LANES), jnp.float32)
        for z, inner in layers:
            c, d = tiles_of(c_ref, z, groups), tiles_of(d_ref, z, groups)
            keep = z == jnp.where(first, depth - 1, 0)
            x = [jnp.where(keep, x[t], d[t] + c[t] * x[t]) for t in range(groups)]
            f = [p + OMEGA * (x[t] - p) for t, p in enumerate(tiles_of(p_ref, z, groups))]
            put_tiles(f_ref, z, f)
            for t in range(groups):
                m = groups * inner + t
                out = jnp.where(slot == m, pltpu.roll(f[t], (2 * m) % LANES, 1), out)
            ends_ref[0, pl.ds(z, 1), :] = f[0][0:1, :]
            ends_ref[1, pl.ds(z, 1), :] = f[-1][SUB - 1 : SUB, :]
        rim_ref[chunk] = out
        return x

    x = [x_end[SUB * t : SUB * (t + 1), :] for t in range(groups)]
    chunked(depth, groups, jnp.logical_not(first), body, x)


def eliminate_again_kernel(
    b_ref, c_ref, inv_ref, f_ref, rows_ref, rim_ref, west_ref, east_ref, forward_ref, backward_ref,
    d_ref, face_ref, add_rows, add_rim,
):
    depth, width, _ = b_ref.shape
    groups = width // SUB
    first = lax.axis_index("gz") == 0
    lane, row = lane_iota(), row_iota()
    even = (lane & 1) == 0
    add_rows[0] = rows_ref[0] * west_ref[...]
    add_rows[1] = rows_ref[1] * east_ref[...]
    for t in range(rim_ref.shape[0]):
        south, north = split_rims(forward_ref[t], backward_ref[t], first)
        add_rim[t] = rim_ref[t] * join_rims(south, north, even)
    rim_lane = (lane == 0) | (lane == LANES - 1)

    def body(chunk, layers, carried):
        tile_b = add_rim[chunk]
        g = carried
        for z, inner in layers:
            b, inv, c = (tiles_of(ref, z, groups) for ref in (b_ref, inv_ref, c_ref))
            for x in range(groups):
                b[x] = b[x] + jnp.where(rim_lane, rim_part(tile_b, inner, x, groups), 0.0)
            for x, which, at in ((0, 0, 0), (groups - 1, 1, SUB - 1)):
                b[x] = b[x] + jnp.where(row == at, add_rows[which, pl.ds(z, 1), :], 0.0)
            g = [b[x] + carried[x] for x in range(groups)]
            put_tiles(d_ref, z, [g[x] * inv[x] for x in range(groups)])
            carried = [c[x] * g[x] for x in range(groups)]
        put_tiles(face_ref, 0, g)
        return carried

    zero = [jnp.zeros((SUB, LANES), jnp.float32) for _ in range(groups)]
    chunked(depth, groups, first, body, zero)
    face_ref[1] = f_ref[jnp.where(first, depth - 1, 0)]


def back_again_kernel(
    c_ref, d_ref, p_ref, coef_ref, face_ref, other_ref, f_ref, rim_ref, ends_ref, flux_ref
):
    first = lax.axis_index("gz") == 0
    slot = rim_slot()
    own, other = face_ref[0], other_ref[0]
    x = coef_ref[0] * own + coef_ref[1] * other
    y = coef_ref[2] * other + coef_ref[1] * own
    mine, theirs = face_ref[1], other_ref[1]
    mine = mine + OMEGA * (x - mine)
    theirs = theirs + OMEGA * (y - theirs)
    flux_ref[...] = coef_ref[3] * (mine - theirs)
    finish_back(x, c_ref, d_ref, p_ref, f_ref, rim_ref, ends_ref, first, slot)


def residual_kernel(
    source_ref, storage_ref, tz_ref, tx_ref, ty_ref, f_ref, flux_ref, r_ref, f_hbm, sem
):
    depth, width, _ = r_ref.shape
    out = pltpu.make_async_copy(f_ref, f_hbm, sem)
    out.start()
    first = lax.axis_index("gz") == 0

    def layer(z, below):
        p = f_ref[z]
        cx, cy = interior_couplings(tx_ref[z], ty_ref[z])
        above = tz_ref[z] * (p - f_ref[jnp.minimum(z + 1, depth - 1)])
        gx = cx * (p - pltpu.roll(p, width - 1, 0))
        gy = cy * (p - pltpu.roll(p, LANES - 1, 1))
        r = source_ref[z] - storage_ref[z] * p - (gx - pltpu.roll(gx, 1, 0))
        r_ref[z] = r - (gy - pltpu.roll(gy, 1, 1)) - (above - below)
        return above

    lax.fori_loop(0, depth, layer, jnp.zeros_like(flux_ref[...]), unroll=4)
    end = jnp.where(first, depth - 1, 0)
    r_ref[end] = r_ref[end] - flux_ref[...]
    out.wait()


def rims_kernel(
    r_ref, rows_ref, rim_ref, own_ref, ends_ref, west_ref, east_ref, forward_ref, backward_ref, out_ref
):
    depth, width, _ = r_ref.shape
    groups = width // SUB
    first = lax.axis_index("gz") == 0
    lane, row = lane_iota(), row_iota()
    even = (lane & 1) == 0
    rim_lane = (lane == 0) | (lane == LANES - 1)
    south, north = split_rims(forward_ref[0], backward_ref[0], first)
    more = rim_ref[0] * (join_rims(south, north, even) - own_ref[0])
    west = rows_ref[0] * (west_ref[...] - ends_ref[0])
    east = rows_ref[1] * (east_ref[...] - ends_ref[1])
    for z in range(depth):
        tiles = tiles_of(r_ref, z, groups)
        for x in range(groups):
            tiles[x] = tiles[x] + jnp.where(rim_lane, rim_part(more, z, x, groups), 0.0)
        tiles[0] = tiles[0] + jnp.where(row == 0, west[z : z + 1, :], 0.0)
        tiles[-1] = tiles[-1] + jnp.where(row == SUB - 1, east[z : z + 1, :], 0.0)
        put_tiles(out_ref, z, tiles)


def ring(value, axis, step):
    count = lax.axis_size(axis)
    return lax.ppermute(value, axis, [(i, (i + step) % count) for i in range(count)])


def snake(value, step):
    count = lax.axis_size("ay")
    order = list(range(count)) + [2 * count - 1 - i for i in range(count)]
    total = len(order)
    pairs = [(order[i], order[(i + step) % total]) for i in range(total)]
    return lax.ppermute(value, ("gz", "ay"), pairs)


def two_blocks(source, pressure, storage, trans_z, trans_x, trans_y):
    depth, width, length = pressure.shape
    groups = width // SUB
    chunk = LANES // 2 // groups
    steps = depth // chunk
    f32 = jnp.float32

    def shape(*dims):
        return jax.ShapeDtypeStruct(dims, f32)

    block = shape(depth, width, length)
    face = shape(width, length)
    rim = shape(steps, SUB, LANES)
    ends = shape(2, depth, length)
    whole = pl.BlockSpec(memory_space=pltpu.VMEM)
    far = pl.BlockSpec(memory_space=pltpu.HBM)
    part = pl.BlockSpec((chunk, width, length), lambda i: (i, 0, 0))
    part_rim = pl.BlockSpec((1, SUB, LANES), lambda i: (i, 0, 0))
    part_ends = pl.BlockSpec((2, chunk, length), lambda i: (0, i, 0))
    part_end = pl.BlockSpec((chunk, length), lambda i: (i, 0))

    def cost(flops, nbytes):
        return pl.CostEstimate(flops=flops, bytes_accessed=nbytes, transcendentals=0)

    size = depth * width * length
    params = pltpu.CompilerParams(vmem_limit_bytes=LIMIT)

    rims, east, west, pressure, trans_x, trans_y = pl.pallas_call(
        pack_inputs_kernel,
        in_specs=[far] * 3,
        out_specs=[whole] * 6,
        out_shape=[shape(2, steps, SUB, LANES), ends, shape(depth, length), block, block, block],
        scratch_shapes=[pltpu.SemaphoreType.DMA((2 * steps + 1,))],
        compiler_params=params,
        cost_estimate=cost(4 * size, 24 * size),
        name="pack_inputs",
    )(pressure, trans_x, trans_y)

    from_west = ring(east, "ax", 1)
    from_east = ring(west, "ax", -1)
    forward = snake(rims, 1)
    backward = snake(rims, -1)

    s, b, source, storage, cz = pl.pallas_call(
        prepare_kernel,
        in_specs=[far] * 3 + [whole] * 3,
        out_specs=[whole] * 5,
        out_shape=[block] * 5,
        scratch_shapes=[pltpu.SemaphoreType.DMA((2 * steps + 1,))],
        compiler_params=params,
        cost_estimate=cost(20 * size, 36 * size),
        name="prepare",
    )(source, storage, trans_z, pressure, trans_x, trans_y)

    scratch = [pltpu.VMEM((2, depth, length), f32), pltpu.VMEM((steps, SUB, LANES), f32)]
    c, inv, d, faces, rows, coupling = pl.pallas_call(
        eliminate_kernel,
        in_specs=[whole] * 9,
        out_specs=[whole] * 6,
        out_shape=[block, block, block, shape(3, width, length), ends, rim],
        scratch_shapes=scratch,
        compiler_params=params,
        cost_estimate=cost(30 * size, 24 * size),
        name="eliminate",
    )(s, b, cz, rims, east, from_west, from_east, forward, backward)

    others = ring(faces, "gz", 1)
    field, coefs, rims, edges = pl.pallas_call(
        back_kernel,
        in_specs=[whole] * 5,
        out_specs=[whole] * 4,
        out_shape=[block, shape(4, width, length), rim, ends],
        compiler_params=params,
        cost_estimate=cost(10 * size, 16 * size),
        name="back",
    )(c, d, pressure, faces, others)

    from_west = ring(edges[1], "ax", 1)
    from_east = ring(edges[0], "ax", -1)
    forward = snake(rims, 1)
    backward = snake(rims, -1)

    b = pl.pallas_call(
        line_kernel,
        in_specs=[whole] * 4,
        out_specs=whole,
        out_shape=block,
        compiler_params=params,
        cost_estimate=cost(16 * size, 20 * size),
        name="line",
    )(source, field, trans_x, trans_y)

    d, faces = pl.pallas_call(
        eliminate_again_kernel,
        in_specs=[whole] * 10,
        out_specs=[whole] * 2,
        out_shape=[block, shape(2, width, length)],
        scratch_shapes=scratch,
        compiler_params=params,
        cost_estimate=cost(10 * size, 16 * size),
        name="eliminate_again",
    )(b, c, inv, field, rows, coupling, from_west, from_east, forward, backward)

    others = ring(faces, "gz", 1)
    field, rims, edges, flux = pl.pallas_call(
        back_again_kernel,
        in_specs=[whole] * 6,
        out_specs=[whole] * 4,
        out_shape=[block, rim, ends, face],
        compiler_params=params,
        cost_estimate=cost(10 * size, 16 * size),
        name="back_again",
    )(c, d, field, coefs, faces, others)

    from_west = ring(edges[1], "ax", 1)
    from_east = ring(edges[0], "ax", -1)
    forward = snake(rims, 1)
    backward = snake(rims, -1)

    r, smoothed = pl.pallas_call(
        residual_kernel,
        in_specs=[whole] * 7,
        out_specs=[whole, far],
        out_shape=[block, block],
        scratch_shapes=[pltpu.SemaphoreType.DMA],
        compiler_params=params,
        cost_estimate=cost(20 * size, 28 * size),
        name="residual",
    )(source, storage, cz, trans_x, trans_y, field, flux)

    r = pl.pallas_call(
        rims_kernel,
        grid=(steps,),
        in_specs=[
            part, part_ends, part_rim, part_rim, part_ends, part_end, part_end, part_rim, part_rim
        ],
        out_specs=part,
        out_shape=block,
        compiler_params=params,
        cost_estimate=cost(4 * size, 8 * size),
        name="rims",
    )(r, rows, coupling, rims, edges, from_west, from_east, forward, backward)
    return smoothed, r


def body(*args):
    depth, width, length = args[0].shape
    groups = width // SUB
    fits = width % SUB == 0 and length == LANES and LANES // 2 % groups == 0
    if lax.axis_size("gz") == 2 and fits and depth % (LANES // 2 // groups) == 0:
        return two_blocks(*args)
    return many_blocks(*args)


def solution(mesh):
    spec = P("gz", "ax", "ay")
    return jax.shard_map(
        body, mesh=mesh, in_specs=(spec,) * 6, out_specs=(spec, spec), check_vma=False
    )
```
